1024 devices in a mesh: seq: 64 (over z, y_hi), head: 16 (over x, y_lo, core).
Axes of the slice: x: 4, y: 4 (y_hi: 2, y_lo: 2; y = y_hi * 2 + y_lo), z: 32, core: 2. Of those that a mesh axis runs over, the one named last changes fastest.
Arguments:
- q_in: bfloat16 [8192, 2048], P(('seq', 'head')), may hold values from -52 to 52
- k_in: bfloat16 [8192, 2048], P(('seq', 'head')), may hold values from -6 to 6
- v_in: bfloat16 [8192, 2048], P(('seq', 'head')), may hold values from -6 to 6
- grad_out: bfloat16 [8192, 2048], P(('seq', 'head')), may hold values from -6 to 6
- positions: int32 [3, 8192], P(None, 'seq'), may hold values from 0 to 79, as said below
- views: int32 [8192], replicated, may hold values from 0 to 5, as said below
- adjacency: int32 [6, 2], replicated, may hold values from 0 to 5, as said below
Outputs:
- attended: bfloat16 [8192, 2048], P('seq', 'head')
- grad_q: bfloat16 [8192, 2048], P('seq', 'head')
- grad_k: bfloat16 [8192, 2048], P('seq', 'head')
- grad_v: bfloat16 [8192, 2048], P('seq', 'head')
The draws below stay inside these ranges and needn't reach their ends.
Inputs may be any that keep to these rules, and one draw needn't show every extreme that they name: `positions`: time ids lie below 16, height ids below 44, width ids below 80. `views`: never decreasing, starting at 0; a view changes only at a multiple of 128 rows; each view holds the rows of 10 devices or of one device more, and which views hold one more is drawn. `adjacency`: the two entries of a view are distinct other views; the relation is symmetric and joins all views in one closed cycle.
All inputs are finite; a program needn't handle non-finite values.
Results may differ from the reference program's by a relative error of at most 0.025.
Values may be sent and summed in bfloat16 or wider, within the bound.
A program may use at most 32 MiB of HBM per device.

```python
import jax
import jax.numpy as jnp
from jax import lax

HD = 128
HEADS = 16
VIEWS = 6
TOK_DEV = 128
TOKENS = 8192


def query_key_pair(key):
    shape = (TOKENS, HEADS * HD)
    keys = jnp.clip(jax.random.normal(jax.random.fold_in(key, 11), shape, jnp.float32), -6.0, 6.0)
    queries = jnp.clip(jax.random.normal(jax.random.fold_in(key, 12), shape, jnp.float32), -6.0, 6.0)
    return (queries, keys)


def draw_q_in(key, part):
    return query_key_pair(key)[0].astype(jnp.bfloat16)


def draw_k_in(key, part):
    return query_key_pair(key)[1].astype(jnp.bfloat16)


def draw_positions(key, part):
    frames = jax.random.randint(jax.random.fold_in(key, 31), (TOKENS,), 0, 16, jnp.int32)
    height = jax.random.randint(jax.random.fold_in(key, 32), (TOKENS,), 0, 44, jnp.int32)
    width = jax.random.randint(jax.random.fold_in(key, 33), (TOKENS,), 0, 80, jnp.int32)
    stacked = jnp.stack([frames, height, width], axis=0)
    stacked = stacked.at[:, TOKENS // 2].set(jnp.array([15, 43, 79], jnp.int32))
    stacked = stacked.at[:, 0].set(jnp.zeros((3,), jnp.int32))
    return stacked


def draw_views(key, part):
    devices = TOKENS // TOK_DEV
    order = jax.random.permutation(jax.random.fold_in(key, 41), VIEWS).astype(jnp.int32)
    extra = (order < devices % VIEWS).astype(jnp.int32)
    counts = devices // VIEWS + extra
    ends = jnp.cumsum(counts).astype(jnp.int32)
    device_of = (jnp.arange(TOKENS, dtype=jnp.int32) // TOK_DEV).astype(jnp.int32)
    return jnp.sum((device_of[:, None] >= ends[None, :]).astype(jnp.int32), axis=1).astype(jnp.int32)


def draw_adjacency(key, part):
    order = jax.random.permutation(jax.random.fold_in(key, 21), VIEWS).astype(jnp.int32)
    before = jnp.roll(order, 1)
    after = jnp.roll(order, -1)
    table = jnp.zeros((VIEWS, 2), jnp.int32)
    return table.at[order].set(jnp.stack([before, after], axis=1))


def steps_of(stream_key, extent, shards, smallest, high):
    loudness = 1.0
    for axis_at, blocks in shards:
        steps = jax.random.uniform(jax.random.fold_in(jax.random.fold_in(stream_key, 6), axis_at), (blocks,), jnp.float32, smallest / len(shards), high / len(shards))
        loudness = loudness * jnp.repeat(jnp.exp(steps), extent[axis_at] // blocks).reshape((-1,) + (1,) * (len(extent) - 1 - axis_at))
    return loudness


def noise(own_key, shape, scale, bound, shards=(), kind=jnp.bfloat16):
    result = scale * jax.random.normal(own_key, shape, jnp.float32)
    if shards:
        result = result * steps_of(own_key, shape, shards, -0.22, 0.18)
    return jnp.clip(result, -bound, bound).astype(kind)


def setup_inputs(seed: int = 0) -> dict:
    splits = jax.random.split(jax.random.key(seed), 8)
    q_in = draw_q_in(jax.random.fold_in(splits[7], 71), 0)
    k_in = draw_k_in(jax.random.fold_in(splits[7], 71), 0)
    v_in = noise(splits[2], (TOKENS, HEADS * HD), 1.0, 6.0, ((0, 1024),))
    grad_out = noise(splits[3], (TOKENS, HEADS * HD), 1.0, 6.0, ((0, 1024),))
    positions = draw_positions(jax.random.fold_in(splits[7], 71), 0)
    views = draw_views(jax.random.fold_in(splits[7], 71), 0)
    adjacency = draw_adjacency(jax.random.fold_in(splits[7], 71), 0)
    return dict(q_in=q_in, k_in=k_in, v_in=v_in, grad_out=grad_out, positions=positions, views=views, adjacency=adjacency)


NEG = -1e30
THETA = 10000.0


def rope_tables(positions, width):
    side = width // 6 * 2
    first = width - 2 * side
    parts = []
    for row, group in ((0, first), (1, side), (2, side)):
        steps = jnp.arange(group // 2, dtype=jnp.float32)
        inverse = THETA ** (-2.0 * steps / group)
        parts.append(positions[row].astype(jnp.float32)[:, None] * inverse[None, :])
    angles = jnp.concatenate(parts, axis=1)
    return jnp.cos(angles), jnp.sin(angles)


def rotate(values, cosine, sine, sign):
    half = values.shape[-1] // 2
    first = values[..., :half]
    second = values[..., half:]
    return jnp.concatenate([first * cosine - sign * second * sine, sign * first * sine + second * cosine], axis=-1)


def neighbours(view_ids, adjacency):
    count = adjacency.shape[0]
    match = view_ids[:, None] == jnp.arange(count, dtype=jnp.int32)[None, :]
    near_one = jnp.sum(jnp.where(match, adjacency[None, :, 0], 0), axis=1).astype(jnp.int32)
    near_two = jnp.sum(jnp.where(match, adjacency[None, :, 1], 0), axis=1).astype(jnp.int32)
    return near_one, near_two


def reference(q_in, k_in, v_in, grad_out, positions, views, adjacency):
    scale = HD ** -0.5
    cosine, sine = rope_tables(positions, HD)
    near_one, near_two = neighbours(views, adjacency)
    other = views[None, :]
    allowed = (other == views[:, None]) | (other == near_one[:, None]) | (other == near_two[:, None])

    def one_head(head):
        start = head * HD

        def take(array):
            return lax.dynamic_slice_in_dim(array, start, HD, 1)

        query = rotate(take(q_in).astype(jnp.float32), cosine, sine, 1.0).astype(jnp.bfloat16)
        keyrot = rotate(take(k_in).astype(jnp.float32), cosine, sine, 1.0).astype(jnp.bfloat16)
        values = take(v_in)
        grads = take(grad_out)
        scores = jnp.dot(query, keyrot.T, preferred_element_type=jnp.float32) * scale
        scores = jnp.where(allowed, scores, NEG)
        top = jnp.max(scores, axis=1)
        weights = jnp.where(allowed, jnp.exp(scores - top[:, None]), 0.0)
        total = jnp.sum(weights, axis=1)
        output = jnp.dot(weights.astype(jnp.bfloat16), values, preferred_element_type=jnp.float32) / total[:, None]
        level = top + jnp.log(total)
        delta = jnp.sum(grads.astype(jnp.float32) * output, axis=1)
        probs = jnp.where(allowed, jnp.exp(scores - level[:, None]), 0.0)
        dprobs = jnp.dot(grads, values.T, preferred_element_type=jnp.float32)
        dscores = (probs * (dprobs - delta[:, None])).astype(jnp.bfloat16)
        grad_query = jnp.dot(dscores, keyrot, preferred_element_type=jnp.float32) * scale
        grad_key = jnp.dot(dscores.T, query, preferred_element_type=jnp.float32) * scale
        grad_value = jnp.dot(probs.astype(jnp.bfloat16).T, grads, preferred_element_type=jnp.float32)
        return (output.astype(jnp.bfloat16),
                rotate(grad_query, cosine, sine, -1.0).astype(jnp.bfloat16),
                rotate(grad_key, cosine, sine, -1.0).astype(jnp.bfloat16),
                grad_value.astype(jnp.bfloat16))

    results = lax.map(one_head, jnp.arange(HEADS, dtype=jnp.int32))

    def merge_heads(stack):
        return jnp.transpose(stack, (1, 0, 2)).reshape(TOKENS, HEADS * HD)

    return (merge_heads(results[0]), merge_heads(results[1]), merge_heads(results[2]), merge_heads(results[3]))
```

```python
import functools

import jax
import jax.numpy as jnp
from jax import lax
from jax.experimental import pallas as pl
from jax.experimental.pallas import tpu as pltpu
from jax.sharding import PartitionSpec as P

HD = 128
NEG = -1e30
THETA = 10000.0
MESH = pl.DeviceIdType.MESH
SKEW = 1


def rope_tables(positions, width):
    side = width // 6 * 2
    first = width - 2 * side
    parts = []
    for row, group in ((0, first), (1, side), (2, side)):
        steps = jnp.arange(group // 2, dtype=jnp.float32)
        inverse = THETA ** (-2.0 * steps / group)
        parts.append(positions[row].astype(jnp.float32)[:, None] * inverse[None, :])
    angles = jnp.concatenate(parts, axis=1)
    return (jnp.cos(angles), jnp.sin(angles))


def rotate(values, cosine, sine, sign):
    half = values.shape[-1] // 2
    first = values[..., :half]
    second = values[..., half:]
    return jnp.concatenate(
        [first * cosine - sign * second * sine, sign * first * sine + second * cosine], axis=-1
    )


def dot_nt(a, b):
    return lax.dot_general(a, b, (((1,), (1,)), ((), ())), preferred_element_type=jnp.float32)


def dot_nn(a, b):
    return lax.dot_general(a, b, (((1,), (0,)), ((), ())), preferred_element_type=jnp.float32)


def dot_tn(a, b):
    return lax.dot_general(a, b, (((0,), (0,)), ((), ())), preferred_element_type=jnp.float32)


def kernel(
    seq_count, toks,
    k_ref, v_ref, q_ref, d_ref, bias_ref,
    att_ref, grad_ref,
    ring, gbuf, acc, stat, racc, rstat, lring, glse, dqt, dkv, attbuf, hsend, hrecv,
    a2a_send, a2a_recv, g_send, g_recv, g_own, r_send, r_recv, l_send, l_recv,
    p_send, p_recv, gl_send, gl_recv, gl_own, at_send, at_recv, h_send, h_recv,
):
    T = toks
    SUB = T // 16
    NP = seq_count // 4
    HALF = NP // 2
    scale = HD ** (-0.5)
    s = lax.axis_index("seq")
    hd = lax.axis_index("head")
    pair = s // 4
    r = (s // 2) % 2
    yh = s % 2
    xh = hd // 8
    xl = (hd // 4) % 2
    low = hd % 4
    j = 2 * xh + yh
    head = (2 * r + xl) * 4 + low
    base = 4 * pair
    diag = xh == r

    right = ((s + 4) % seq_count, hd)
    left = ((s + seq_count - 4) % seq_count, hd)

    def member(i):
        return (base + 2 * r + i % 2, (2 * (i // 2) + xl) * 4 + low)

    def home(i):
        return (base + i, head)

    def home_sender(i):
        return (base + 2 * xh + i % 2, (2 * (i // 2) + xl) * 4 + low)

    def a2a_dest(h):
        xo = h // 4
        return (base + 2 * (xo // 2) + yh, (2 * r + xo % 2) * 4 + h % 4)

    def is_me(dev):
        return jnp.logical_and(dev[0] == s, dev[1] == hd)

    barrier = pltpu.get_barrier_semaphore()

    @pl.loop(0, 16)
    def _(i):
        src = (base + j, i)

        @pl.when(jnp.logical_not(is_me(src)))
        def _():
            pl.semaphore_signal(barrier, inc=1, device_id=src, device_id_type=MESH)

    for i in range(4):
        src = home_sender(i)

        @pl.when(jnp.logical_not(is_me(src)))
        def _():
            pl.semaphore_signal(barrier, inc=1, device_id=src, device_id_type=MESH)

    for dev in (right, left):
        pl.semaphore_signal(barrier, inc=1, device_id=dev, device_id_type=MESH)
    peers = []
    for delta in (1, 2, 3):
        i = (j + delta) % 4
        peers.append(i)
        pl.semaphore_signal(barrier, inc=1, device_id=member((j - delta + 4) % 4), device_id_type=MESH)
    pl.semaphore_wait(barrier, 25 - 2 * diag.astype(jnp.int32))

    inputs = (k_ref, v_ref, q_ref, d_ref)

    def a2a_remote(t, h):
        return pltpu.make_async_remote_copy(
            src_ref=inputs[t].at[:, pl.ds(pl.multiple_of(h * HD, HD), HD)],
            dst_ref=ring.at[t, pl.ds(pl.multiple_of(hd * SUB, SUB), SUB), :],
            send_sem=a2a_send.at[t], recv_sem=a2a_recv.at[t],
            device_id=a2a_dest(h), device_id_type=MESH,
        )

    def a2a_local(t, h):
        return pltpu.make_async_copy(
            inputs[t].at[:, pl.ds(pl.multiple_of(h * HD, HD), HD)],
            ring.at[t, pl.ds(pl.multiple_of(hd * SUB, SUB), SUB), :],
            a2a_recv.at[t],
        )

    for t in range(4):
        @pl.loop(0, 16)
        def _(h):
            mine = is_me(a2a_dest(h))

            @pl.when(mine)
            def _():
                a2a_local(t, h).start()

            @pl.when(jnp.logical_not(mine))
            def _():
                a2a_remote(t, h).start()

    def rows(i):
        return pl.ds(i * T, T)

    def own(t):
        return ring.at[t, rows(0), :]

    def wait_bytes(ref, sem):
        pltpu.make_async_copy(ref, ref, sem).wait()

    def ring_copy(t, way, step):
        if way == 0:
            src = jnp.maximum(2 * step - 3, 0)
            dst = 2 * step - 1
        else:
            src = 2 * step - 2
            dst = jnp.minimum(2 * step, 2 * HALF - 1)
        return pltpu.make_async_remote_copy(
            src_ref=ring.at[t, pl.ds(pl.multiple_of(src * T, T), T), :],
            dst_ref=ring.at[t, pl.ds(pl.multiple_of(dst * T, T), T), :],
            send_sem=r_send.at[t, way, step - 1], recv_sem=r_recv.at[t, way, step - 1],
            device_id=right if way == 0 else left, device_id_type=MESH,
        )

    def lse_copy(way, step):
        if way == 0:
            src = jnp.maximum(2 * step - 3, 0)
            dst = 2 * step - 1
        else:
            src = 2 * step - 2
            dst = jnp.minimum(2 * step, 2 * HALF - 1)
        return pltpu.make_async_remote_copy(
            src_ref=lring.at[src], dst_ref=lring.at[dst],
            send_sem=l_send.at[way, step - 1], recv_sem=l_recv.at[way, step - 1],
            device_id=right if way == 0 else left, device_id_type=MESH,
        )

    def group_copy(t, n):
        return pltpu.make_async_remote_copy(
            src_ref=own(t), dst_ref=gbuf.at[t, pl.ds(pl.multiple_of(j * T, T), T), :],
            send_sem=g_send.at[t, n], recv_sem=g_recv.at[t, n],
            device_id=member(peers[n]), device_id_type=MESH,
        )

    def group_own(t):
        return pltpu.make_async_copy(
            own(t), gbuf.at[t, pl.ds(pl.multiple_of(j * T, T), T), :], g_own.at[t]
        )

    for t in (0, 1):
        wait_bytes(own(t), a2a_recv.at[t])
        for way in (0, 1):
            ring_copy(t, way, jnp.int32(1)).start()
    for t in (2, 3):
        wait_bytes(own(t), a2a_recv.at[t])
    for t in (2, 3, 0, 1):
        for n in range(3):
            group_copy(t, n).start()
        group_own(t).start()

    def group_wait(t):
        for n in range(3):
            group_copy(t, n).wait_recv()
        group_own(t).wait()

    group_wait(2)

    def fwd(start, size, bias, first):
        keys = ring[0, pl.ds(start, size), :]
        vals = ring[1, pl.ds(start, size), :]
        st = dot_nt(keys, gbuf[2]) * scale
        st = st + bias
        peak = jnp.max(st, axis=0, keepdims=True)
        if first:
            top = peak
        else:
            top = jnp.maximum(stat[0:1, :], peak)
        e = jnp.exp(st - top)
        total = jnp.sum(e, axis=0, keepdims=True)
        out = dot_tn(vals, e.astype(jnp.bfloat16))
        if first:
            stat[1:2, :] = total
            acc[...] = out
        else:
            shrink = jnp.exp(stat[0:1, :] - top)
            stat[1:2, :] = stat[1:2, :] * shrink + total
            acc[...] = acc[...] * shrink + out
        stat[0:1, :] = top

    def bias_of(step):
        one = jnp.broadcast_to(bias_ref[2 * step - 1], (T, 4 * T))
        two = jnp.broadcast_to(bias_ref[2 * step], (T, 4 * T))
        return jnp.concatenate([one, two], axis=0)

    LAST = 2 * HALF - 1
    stat[...] = jnp.zeros_like(stat)
    fwd(0, T, bias_ref[0], True)

    def forward_ring(pairs, step):
        for t, way in pairs:
            ring_copy(t, way, step).wait_recv()

            @pl.when(step + 1 < HALF)
            def _():
                ring_copy(t, way, step + 1).start()

            if (t % 2) == way:
                @pl.when(step + 1 == HALF)
                def _():
                    ring_copy(t, way, step + 1).start()

    @pl.loop(1, HALF)
    def _(step):
        forward_ring(((0, 0), (0, 1), (1, 0), (1, 1)), step)
        fwd(pl.multiple_of((2 * step - 1) * T, T), 2 * T, bias_of(step), False)

    for t in (2, 3):
        for way in (0, 1):
            ring_copy(t, way, jnp.int32(1)).start()
    ring_copy(0, 0, jnp.int32(HALF)).wait_recv()
    ring_copy(1, 1, jnp.int32(HALF)).wait_recv()
    fwd(LAST * T, T, bias_ref[LAST], False)

    def part_copy(which, n):
        lanes = pl.ds(pl.multiple_of(peers[n] * T, T), T)
        src, dst = ((acc, racc), (stat, rstat))[which]
        return pltpu.make_async_remote_copy(
            src_ref=src.at[:, lanes], dst_ref=dst.at[n],
            send_sem=p_send.at[which, n], recv_sem=p_recv.at[which, n],
            device_id=member(peers[n]), device_id_type=MESH,
        )

    for n in range(3):
        part_copy(1, n).start()
        part_copy(0, n).start()
    for t in (3, 0, 1):
        group_wait(t)
    mine = pl.ds(pl.multiple_of(j * T, T), T)
    own_stat = stat[:, mine]
    own_acc = acc[:, mine]
    for n in range(3):
        part_copy(1, n).wait_recv()
        part_copy(0, n).wait_recv()
    stats = [own_stat] + [rstat[n] for n in range(3)]
    top = stats[0][0:1]
    for item in stats[1:]:
        top = jnp.maximum(top, item[0:1])
    total = jnp.zeros_like(top)
    out = jnp.zeros_like(own_acc)
    for n, item in enumerate(stats):
        weight = jnp.exp(item[0:1] - top)
        total = total + item[1:2] * weight
        out = out + (own_acc if n == 0 else racc[n - 1]) * weight
    out = out / total
    lse = top + jnp.log(total)
    dt = jnp.transpose(ring[3, 0:T, :].astype(jnp.float32))
    delta = jnp.sum(dt * out, axis=0, keepdims=True)
    lring[0, 0:1, :] = lse
    lring[0, 1:2, :] = delta
    lring[0, 2:8, :] = jnp.zeros((6, T), jnp.float32)
    attbuf[...] = jnp.transpose(out).astype(jnp.bfloat16)
    for way in (0, 1):
        lse_copy(way, jnp.int32(1)).start()

    def glse_copy(n):
        return pltpu.make_async_remote_copy(
            src_ref=lring.at[0], dst_ref=glse.at[:, mine],
            send_sem=gl_send.at[n], recv_sem=gl_recv.at[n],
            device_id=member(peers[n]), device_id_type=MESH,
        )

    glse_own = pltpu.make_async_copy(lring.at[0], glse.at[:, mine], gl_own)
    for n in range(3):
        glse_copy(n).start()
    glse_own.start()

    def att_remote():
        return pltpu.make_async_remote_copy(
            src_ref=attbuf, dst_ref=att_ref, send_sem=at_send, recv_sem=at_recv,
            device_id=home(j), device_id_type=MESH,
        )

    att_local = pltpu.make_async_copy(attbuf, att_ref, at_recv)
    att_mine = is_me(home(j))

    @pl.when(att_mine)
    def _():
        att_local.start()

    @pl.when(jnp.logical_not(att_mine))
    def _():
        att_remote().start()

    def grad_q(start, size, bias, first):
        keys = ring[0, pl.ds(start, size), :]
        vals = ring[1, pl.ds(start, size), :]
        st = dot_nt(keys, gbuf[2]) * scale
        p = jnp.exp(st + (bias - glse[0:1, :]))
        dp = dot_nt(vals, gbuf[3])
        ds = (p * (dp - glse[1:2, :])).astype(jnp.bfloat16)
        part = dot_tn(keys, ds)
        if first:
            dqt[...] = part
        else:
            dqt[...] += part

    def grad_kv(slot, first):
        start = slot * T if isinstance(slot, int) else pl.multiple_of(slot * T, T)
        queries = ring[2, pl.ds(start, T), :]
        grads = ring[3, pl.ds(start, T), :]
        level = lring[slot, 0:1, :]
        delta = lring[slot, 1:2, :]
        st = dot_nt(gbuf[0], queries) * scale
        dp = dot_nt(gbuf[1], grads)
        bias = bias_ref[slot]
        shift = [
            jnp.broadcast_to(bias[:, i * T:(i + 1) * T] - level, (T, T)) for i in range(4)
        ]
        p = jnp.exp(st + jnp.concatenate(shift, axis=0))
        ds = (p * (dp - delta)).astype(jnp.bfloat16)
        dv = dot_nn(p.astype(jnp.bfloat16), grads)
        dk = dot_nn(ds, queries)
        if first:
            dkv[0] = dk
            dkv[1] = dv
        else:
            dkv[0] += dk
            dkv[1] += dv

    @pl.loop(1, HALF + SKEW)
    def _(step):
        @pl.when(step < HALF)
        def _():
            forward_ring(((2, 0), (2, 1), (3, 0), (3, 1)), step)

        @pl.when(step == SKEW + 1)
        def _():
            for n in range(3):
                glse_copy(n).wait_recv()
            glse_own.wait()
            grad_q(0, T, bias_ref[0], True)
            grad_q(LAST * T, T, bias_ref[LAST], False)
            grad_kv(0, True)

        @pl.when(step > SKEW)
        def _():
            at = step - SKEW
            for way in (0, 1):
                lse_copy(way, at).wait_recv()

                @pl.when(at + 1 < HALF)
                def _():
                    lse_copy(way, at + 1).start()

            @pl.when(at + 1 == HALF)
            def _():
                lse_copy(0, at + 1).start()

            grad_q(pl.multiple_of((2 * at - 1) * T, T), 2 * T, bias_of(at), False)
            grad_kv(2 * at - 1, False)
            grad_kv(2 * at, False)

    for i in range(4):
        hsend[0, i * T:(i + 1) * T, :] = (
            jnp.transpose(dqt[:, i * T:(i + 1) * T]) * scale
        ).astype(jnp.bfloat16)

    def home_remote(t, i):
        return pltpu.make_async_remote_copy(
            src_ref=hsend.at[t, rows(i), :], dst_ref=hrecv.at[t, j],
            send_sem=h_send.at[t, i], recv_sem=h_recv.at[t, j],
            device_id=home(i), device_id_type=MESH,
        )

    def home_local(t, i):
        return pltpu.make_async_copy(hsend.at[t, rows(i), :], hrecv.at[t, j], h_recv.at[t, j])

    def send_home(t):
        for i in range(4):
            here = is_me(home(i))

            @pl.when(here)
            def _():
                home_local(t, i).start()

            @pl.when(jnp.logical_not(here))
            def _():
                home_remote(t, i).start()

    send_home(0)
    ring_copy(2, 0, jnp.int32(HALF)).wait_recv()
    ring_copy(3, 1, jnp.int32(HALF)).wait_recv()
    lse_copy(0, jnp.int32(HALF)).wait_recv()
    grad_kv(LAST, False)
    hsend[1] = (dkv[0] * scale).astype(jnp.bfloat16)
    hsend[2] = dkv[1].astype(jnp.bfloat16)
    send_home(1)
    send_home(2)

    for t in range(4):
        @pl.loop(0, 16)
        def _(h):
            @pl.when(jnp.logical_not(is_me(a2a_dest(h))))
            def _():
                a2a_remote(t, h).wait_send()

        for n in range(3):
            group_copy(t, n).wait_send()

        @pl.loop(1, HALF)
        def _(step):
            for way in (0, 1):
                ring_copy(t, way, step).wait_send()

        ring_copy(t, t % 2, jnp.int32(HALF)).wait_send()

    @pl.loop(1, HALF)
    def _(step):
        for way in (0, 1):
            lse_copy(way, step).wait_send()

    lse_copy(0, jnp.int32(HALF)).wait_send()
    for n in range(3):
        part_copy(0, n).wait_send()
        part_copy(1, n).wait_send()
        glse_copy(n).wait_send()

    @pl.when(jnp.logical_not(att_mine))
    def _():
        att_remote().wait_send()

    wait_bytes(att_ref, at_recv)
    for t in range(3):
        for i in range(4):
            wait_bytes(hrecv.at[t, i], h_recv.at[t, i])
        whole = hrecv[t, 0].astype(jnp.float32)
        for i in range(1, 4):
            whole = whole + hrecv[t, i].astype(jnp.float32)
        grad_ref[t] = whole
    for t in range(3):
        for i in range(4):
            @pl.when(jnp.logical_not(is_me(home(i))))
            def _():
                home_remote(t, i).wait_send()


def exchange_and_attend(seq_count, toks, keys, values, query, grads, bias):
    NP = seq_count // 4
    HALF = NP // 2
    T = toks
    bf, f32 = jnp.bfloat16, jnp.float32
    dma = pltpu.SemaphoreType.DMA
    vmem = pl.BlockSpec(memory_space=pltpu.VMEM)
    return pl.pallas_call(
        functools.partial(kernel, seq_count, toks),
        out_shape=(
            jax.ShapeDtypeStruct((T, HD), bf),
            jax.ShapeDtypeStruct((3, T, HD), f32),
        ),
        in_specs=[vmem] * 5,
        out_specs=(vmem, vmem),
        scratch_shapes=[
            pltpu.VMEM((4, NP * T, HD), bf),
            pltpu.VMEM((4, 4 * T, HD), bf),
            pltpu.VMEM((HD, 4 * T), f32),
            pltpu.VMEM((8, 4 * T), f32),
            pltpu.VMEM((3, HD, T), f32),
            pltpu.VMEM((3, 8, T), f32),
            pltpu.VMEM((NP, 8, T), f32),
            pltpu.VMEM((8, 4 * T), f32),
            pltpu.VMEM((HD, 4 * T), f32),
            pltpu.VMEM((2, 4 * T, HD), f32),
            pltpu.VMEM((T, HD), bf),
            pltpu.VMEM((3, 4 * T, HD), bf),
            pltpu.VMEM((3, 4, T, HD), bf),
            dma((4,)), dma((4,)),
            dma((4, 3)), dma((4, 3)), dma((4,)),
            dma((4, 2, HALF)), dma((4, 2, HALF)),
            dma((2, HALF)), dma((2, HALF)),
            dma((2, 3)), dma((2, 3)),
            dma((3,)), dma((3,)), dma,
            dma, dma,
            dma((3, 4)), dma((3, 4)),
        ],
        compiler_params=pltpu.CompilerParams(collective_id=0, has_side_effects=True),
    )(keys, values, query, grads, bias)


def on_device(seq_count, q_in, k_in, v_in, grad_out, positions, views, adjacency):
    NP = seq_count // 4
    HALF = NP // 2
    T = positions.shape[1]
    sub = q_in.shape[0]
    s = lax.axis_index("seq")
    hd = lax.axis_index("head")
    cosine, sine = rope_tables(positions, HD)
    own_pos = lax.dynamic_slice_in_dim(positions, hd * sub, sub, axis=1)
    c8, s8 = rope_tables(own_pos, HD)

    def turn(x):
        y = rotate(x.reshape(sub, -1, HD).astype(jnp.float32), c8[:, None], s8[:, None], 1.0)
        return y.astype(jnp.bfloat16).reshape(x.shape)

    pair = s // 4
    j = 2 * (hd // 8) + s % 2
    step = jnp.arange(NP, dtype=jnp.int32)
    offset = jnp.where(step % 2 == 1, -(step + 1) // 2, step // 2)
    other = (pair + offset + NP) % NP * 4 + j
    mine = 4 * pair + jnp.arange(4, dtype=jnp.int32)
    block_views = views.reshape(seq_count, T)[:, 0]
    every = jnp.arange(seq_count, dtype=jnp.int32)

    def view_of(index):
        return jnp.sum(jnp.where(index[:, None] == every[None, :], block_views[None, :], 0), axis=1)

    key_view = view_of(other)
    own_view = view_of(mine)
    match = own_view[:, None] == jnp.arange(adjacency.shape[0], dtype=jnp.int32)[None, :]
    near_one = jnp.sum(jnp.where(match, adjacency[None, :, 0], 0), axis=1)
    near_two = jnp.sum(jnp.where(match, adjacency[None, :, 1], 0), axis=1)
    allow = (
        (key_view[:, None] == own_view[None, :])
        | (key_view[:, None] == near_one[None, :])
        | (key_view[:, None] == near_two[None, :])
    )
    bias = jnp.broadcast_to(jnp.where(allow, 0.0, NEG)[:, :, None], (NP, 4, T)).reshape(NP, 1, 4 * T)

    attended, grads = exchange_and_attend(
        seq_count, T, turn(k_in), v_in, turn(q_in), grad_out, bias
    )
    grad_q = rotate(grads[0], cosine, sine, -1.0).astype(jnp.bfloat16)
    grad_k = rotate(grads[1], cosine, sine, -1.0).astype(jnp.bfloat16)
    return (attended, grad_q, grad_k, grads[2].astype(jnp.bfloat16))


def solution(mesh):
    rows = P(("seq", "head"), None)
    in_specs = (rows, rows, rows, rows, P(None, "seq"), P(), P())
    out = P("seq", "head")
    return jax.shard_map(
        functools.partial(on_device, mesh.shape["seq"]),
        mesh=mesh, in_specs=in_specs, out_specs=(out,) * 4, check_vma=False,
    )
```

```python
import functools

import jax
import jax.numpy as jnp
import numpy as np
from jax import lax
from jax.experimental import pallas as pl
from jax.experimental.pallas import tpu as pltpu
from jax.sharding import PartitionSpec as P

HD = 128
NEG = -1e30
THETA = 10000.0
MESH = pl.DeviceIdType.MESH
SKEW = 1
PIECES = 4


def dot_nt(a, b):
    return lax.dot_general(a, b, (((1,), (1,)), ((), ())), preferred_element_type=jnp.float32)


def dot_nn(a, b):
    return lax.dot_general(a, b, (((1,), (0,)), ((), ())), preferred_element_type=jnp.float32)


def dot_tn(a, b):
    return lax.dot_general(a, b, (((0,), (0,)), ((), ())), preferred_element_type=jnp.float32)


def kernel(
    seq_count, toks,
    k_hbm, v_ref, q_hbm, d_ref, pos_hbm, views_hbm, adj_ref, freq_ref,
    out_ref,
    k_raw, q_raw, k_ref, q_ref, pos_ref, views_ref, bias_ref, ctab, stab, in_sem,
    ring, gbuf, acc, pbuf, stat, racc, rstat, lring, glse, dqt, dkv, attbuf, hsend, hrecv,
    a2a_send, a2a_recv, g_send, g_recv, g_own, r_send, r_recv, l_send, l_recv,
    p_send, p_recv, gl_send, gl_recv, gl_own, at_send, at_recv, h_send, h_recv,
):
    T = toks
    SUB = T // 16
    NP = seq_count // 4
    HALF = NP // 2
    scale = HD ** (-0.5)
    s = lax.axis_index("seq")
    hd = lax.axis_index("head")
    pair = s // 4
    r = (s // 2) % 2
    yh = s % 2
    xh = hd // 8
    xl = (hd // 4) % 2
    low = hd % 4
    j = 2 * xh + yh
    head = (2 * r + xl) * 4 + low
    base = 4 * pair
    diag = xh == r

    right = ((s + 4) % seq_count, hd)
    left = ((s + seq_count - 4) % seq_count, hd)

    def member(i):
        return (base + 2 * r + i % 2, (2 * (i // 2) + xl) * 4 + low)

    def home(i):
        return (base + i, head)

    def home_sender(i):
        return (base + 2 * xh + i % 2, (2 * (i // 2) + xl) * 4 + low)

    def a2a_dest(h):
        xo = h // 4
        return (base + 2 * (xo // 2) + yh, (2 * r + xo % 2) * 4 + h % 4)

    def is_me(dev):
        return jnp.logical_and(dev[0] == s, dev[1] == hd)

    loads = [
        pltpu.make_async_copy(src, dst, in_sem.at[n])
        for n, (src, dst) in enumerate(
            ((pos_hbm, pos_ref), (views_hbm, views_ref), (k_hbm, k_raw), (q_hbm, q_raw))
        )
    ]
    for load in loads:
        load.start()

    barrier = pltpu.get_barrier_semaphore()

    @pl.loop(0, 16)
    def _(i):
        src = (base + j, i)

        @pl.when(jnp.logical_not(is_me(src)))
        def _():
            pl.semaphore_signal(barrier, inc=1, device_id=src, device_id_type=MESH)

    for i in range(4):
        src = home_sender(i)

        @pl.when(jnp.logical_not(is_me(src)))
        def _():
            pl.semaphore_signal(barrier, inc=1, device_id=src, device_id_type=MESH)

    far_right = ((s + 8) % seq_count, hd)
    far_left = ((s + seq_count - 8) % seq_count, hd)
    for dev in (right, left, far_right, far_left):
        pl.semaphore_signal(barrier, inc=1, device_id=dev, device_id_type=MESH)
    peers = []
    for delta in (1, 2, 3):
        i = (j + delta) % 4
        peers.append(i)
        pl.semaphore_signal(barrier, inc=1, device_id=member((j - delta + 4) % 4), device_id_type=MESH)

    loads[0].wait()
    spots = pos_ref[...].astype(jnp.float32)
    spots = jnp.transpose(jnp.concatenate([spots, jnp.zeros((5, T), jnp.float32)], axis=0))
    lane = lax.broadcasted_iota(jnp.int32, (T, HD), 1)
    within = lane % (HD // 2)
    side = HD // 6 * 2 // 2
    first = HD // 2 - 2 * side
    spot = jnp.where(
        within < first, spots[:, 0:1], jnp.where(within < first + side, spots[:, 1:2], spots[:, 2:3])
    )
    angle = spot * freq_ref[...]
    ctab[...] = jnp.cos(angle)
    sine = jnp.sin(angle)
    stab[...] = jnp.where(lane < HD // 2, -sine, sine)
    own_rows = pl.ds(pl.multiple_of(hd * SUB, SUB), SUB)
    c_own = ctab[own_rows, :]
    s_own = stab[own_rows, :]
    for n, src, dst in ((2, k_raw, k_ref), (3, q_raw, q_ref)):
        loads[n].wait()
        for h in range(16):
            x = src[:, h * HD:(h + 1) * HD].astype(jnp.float32)
            y = x * c_own + pltpu.roll(x, HD // 2, 1) * s_own
            dst[:, h * HD:(h + 1) * HD] = y.astype(jnp.bfloat16)
    loads[1].wait()
    views_q = [views_ref[base + i] for i in range(4)]
    nears = []
    for vq in views_q:
        one = jnp.zeros_like(vq)
        two = jnp.zeros_like(vq)
        for v in range(6):
            one = jnp.where(vq == v, adj_ref[0, v], one)
            two = jnp.where(vq == v, adj_ref[1, v], two)
        nears.append((one, two))
    for slot in range(NP):
        offset = -((slot + 1) // 2) if slot % 2 else slot // 2
        vk = views_ref[(pair + offset + NP) % NP * 4 + j]
        for i in range(4):
            allow = (vk == views_q[i]) | (vk == nears[i][0]) | (vk == nears[i][1])
            bias_ref[slot, :, i * T:(i + 1) * T] = jnp.where(allow, 0.0, NEG)
    pl.semaphore_wait(barrier, 27 - 2 * diag.astype(jnp.int32))

    inputs = (k_ref, v_ref, q_ref, d_ref)

    def a2a_remote(t, h):
        return pltpu.make_async_remote_copy(
            src_ref=inputs[t].at[:, pl.ds(pl.multiple_of(h * HD, HD), HD)],
            dst_ref=ring.at[t, pl.ds(pl.multiple_of(hd * SUB, SUB), SUB), :],
            send_sem=a2a_send.at[t], recv_sem=a2a_recv.at[t],
            device_id=a2a_dest(h), device_id_type=MESH,
        )

    def a2a_local(t, h):
        return pltpu.make_async_copy(
            inputs[t].at[:, pl.ds(pl.multiple_of(h * HD, HD), HD)],
            ring.at[t, pl.ds(pl.multiple_of(hd * SUB, SUB), SUB), :],
            a2a_recv.at[t],
        )

    for t in range(4):
        @pl.loop(0, 16)
        def _(h):
            mine = is_me(a2a_dest(h))

            @pl.when(mine)
            def _():
                a2a_local(t, h).start()

            @pl.when(jnp.logical_not(mine))
            def _():
                a2a_remote(t, h).start()

    def rows(i):
        return pl.ds(i * T, T)

    def own(t):
        return ring.at[t, rows(0), :]

    def wait_bytes(ref, sem):
        pltpu.make_async_copy(ref, ref, sem).wait()

    PT = T // PIECES

    def ring_copy(t, way, step, piece):
        if way == 0:
            src = jnp.maximum(2 * step - 3, 0)
            dst = 2 * step - 1
        else:
            src = 2 * step - 2
            dst = jnp.minimum(2 * step, 2 * HALF - 1)
        return pltpu.make_async_remote_copy(
            src_ref=ring.at[t, pl.ds(pl.multiple_of(src * T + piece * PT, PT), PT), :],
            dst_ref=ring.at[t, pl.ds(pl.multiple_of(dst * T + piece * PT, PT), PT), :],
            send_sem=r_send.at[t, way], recv_sem=r_recv.at[t, way, (step - 1) * PIECES + piece],
            device_id=right if way == 0 else left, device_id_type=MESH,
        )

    def ring_start(tensors):
        for piece in range(PIECES):
            for t in tensors:
                for way in (0, 1):
                    ring_copy(t, way, jnp.int32(1), piece).start()

    def ring_last(t):
        for piece in range(PIECES):
            ring_copy(t, t % 2, jnp.int32(HALF), piece).wait_recv()

    def lse_copy(way, step):
        slot = 2 * step - 1 if way == 0 else jnp.minimum(2 * step, 2 * HALF - 1)
        back = jnp.maximum(step - 2, 0)
        src = jnp.maximum(2 * back - 1, 0) if way == 0 else 2 * back
        stride = 4 * jnp.minimum(step, 2)
        seq = (s + stride) % seq_count if way == 0 else (s + seq_count - stride) % seq_count
        return pltpu.make_async_remote_copy(
            src_ref=lring.at[src], dst_ref=lring.at[slot],
            send_sem=l_send.at[way, step - 1], recv_sem=l_recv.at[way, step - 1],
            device_id=(seq, hd), device_id_type=MESH,
        )

    def group_copy(t, n):
        return pltpu.make_async_remote_copy(
            src_ref=own(t), dst_ref=gbuf.at[t, pl.ds(pl.multiple_of(j * T, T), T), :],
            send_sem=g_send.at[t, n], recv_sem=g_recv.at[t, n],
            device_id=member(peers[n]), device_id_type=MESH,
        )

    def group_own(t):
        return pltpu.make_async_copy(
            own(t), gbuf.at[t, pl.ds(pl.multiple_of(j * T, T), T), :], g_own.at[t]
        )

    for t in (0, 1):
        wait_bytes(own(t), a2a_recv.at[t])
    ring_start((0, 1))
    for t in (2, 3):
        wait_bytes(own(t), a2a_recv.at[t])
    for t in (2, 3, 0, 1):
        for n in range(3):
            group_copy(t, n).start()
        group_own(t).start()

    def group_wait(t):
        for n in range(3):
            group_copy(t, n).wait_recv()
        group_own(t).wait()

    group_wait(2)

    def fwd(start, size, bias, first):
        keys = ring[0, pl.ds(start, size), :]
        vals = ring[1, pl.ds(start, size), :]
        st = dot_nt(keys, gbuf[2]) * scale
        st = st + bias
        peak = jnp.max(st, axis=0, keepdims=True)
        if first:
            top = peak
        else:
            top = jnp.maximum(stat[0:1, :], peak)
        e = jnp.exp(st - top)
        total = jnp.sum(e, axis=0, keepdims=True)
        out = dot_tn(vals, e.astype(jnp.bfloat16))
        if first:
            stat[1:2, :] = total
            acc[...] = out
        else:
            shrink = jnp.exp(stat[0:1, :] - top)
            stat[1:2, :] = stat[1:2, :] * shrink + total
            acc[...] = acc[...] * shrink + out
        stat[0:1, :] = top

    def bias_of(step):
        one = jnp.broadcast_to(bias_ref[2 * step - 1], (T, 4 * T))
        two = jnp.broadcast_to(bias_ref[2 * step], (T, 4 * T))
        return jnp.concatenate([one, two], axis=0)

    LAST = 2 * HALF - 1
    stat[...] = jnp.zeros_like(stat)
    fwd(0, T, bias_ref[0], True)

    def forward_ring(pairs, step):
        for piece in range(PIECES):
            for t, way in pairs:
                ring_copy(t, way, step, piece).wait_recv()

                @pl.when(step + 1 < HALF)
                def _():
                    ring_copy(t, way, step + 1, piece).start()

                if (t % 2) == way:
                    @pl.when(step + 1 == HALF)
                    def _():
                        ring_copy(t, way, step + 1, piece).start()

    @pl.loop(1, HALF)
    def _(step):
        forward_ring(((0, 0), (0, 1), (1, 0), (1, 1)), step)

        @pl.when(step + 1 == HALF)
        def _():
            ring_start((2, 3))

        fwd(pl.multiple_of((2 * step - 1) * T, T), 2 * T, bias_of(step), False)

    ring_last(0)
    ring_last(1)
    fwd(LAST * T, T, bias_ref[LAST], False)

    def part_copy(which, n):
        lanes = pl.ds(pl.multiple_of(peers[n] * T, T), T)
        src, dst = ((pbuf, racc), (stat, rstat))[which]
        return pltpu.make_async_remote_copy(
            src_ref=src.at[:, lanes], dst_ref=dst.at[n],
            send_sem=p_send.at[which, n], recv_sem=p_recv.at[which, n],
            device_id=member(peers[n]), device_id_type=MESH,
        )

    pbuf[...] = acc[...].astype(jnp.bfloat16)
    for n in range(3):
        part_copy(1, n).start()
    for n in range(3):
        part_copy(0, n).start()
    for t in (3, 0, 1):
        group_wait(t)
    mine = pl.ds(pl.multiple_of(j * T, T), T)
    own_stat = stat[:, mine]
    own_acc = acc[:, mine]
    for n in range(3):
        part_copy(1, n).wait_recv()
        part_copy(0, n).wait_recv()
    stats = [own_stat] + [rstat[n] for n in range(3)]
    top = stats[0][0:1]
    for item in stats[1:]:
        top = jnp.maximum(top, item[0:1])
    total = jnp.zeros_like(top)
    out = jnp.zeros_like(own_acc)
    for n, item in enumerate(stats):
        weight = jnp.exp(item[0:1] - top)
        total = total + item[1:2] * weight
        out = out + (own_acc if n == 0 else racc[n - 1].astype(jnp.float32)) * weight
    out = out / total
    lse = top + jnp.log(total)
    dt = jnp.transpose(ring[3, 0:T, :].astype(jnp.float32))
    delta = jnp.sum(dt * out, axis=0, keepdims=True)
    lring[0, 0:1, :] = lse
    lring[0, 1:2, :] = delta
    lring[0, 2:8, :] = jnp.zeros((6, T), jnp.float32)
    attbuf[...] = jnp.transpose(out).astype(jnp.bfloat16)
    for step in (1, 2):
        for way in (0, 1):
            lse_copy(way, jnp.int32(step)).start()

    def glse_copy(n):
        return pltpu.make_async_remote_copy(
            src_ref=lring.at[0], dst_ref=glse.at[:, mine],
            send_sem=gl_send.at[n], recv_sem=gl_recv.at[n],
            device_id=member(peers[n]), device_id_type=MESH,
        )

    glse_own = pltpu.make_async_copy(lring.at[0], glse.at[:, mine], gl_own)
    for n in range(3):
        glse_copy(n).start()
    glse_own.start()

    def att_remote():
        return pltpu.make_async_remote_copy(
            src_ref=attbuf, dst_ref=out_ref.at[0], send_sem=at_send, recv_sem=at_recv,
            device_id=home(j), device_id_type=MESH,
        )

    att_local = pltpu.make_async_copy(attbuf, out_ref.at[0], at_recv)
    att_mine = is_me(home(j))

    @pl.when(att_mine)
    def _():
        att_local.start()

    @pl.when(jnp.logical_not(att_mine))
    def _():
        att_remote().start()

    def grad_q(start, size, bias, first):
        keys = ring[0, pl.ds(start, size), :]
        vals = ring[1, pl.ds(start, size), :]
        st = dot_nt(keys, gbuf[2]) * scale
        p = jnp.exp(st + (bias - glse[0:1, :]))
        dp = dot_nt(vals, gbuf[3])
        ds = (p * (dp - glse[1:2, :])).astype(jnp.bfloat16)
        part = dot_tn(keys, ds)
        if first:
            dqt[...] = part
        else:
            dqt[...] += part

    def grad_kv(slot, first):
        start = slot * T if isinstance(slot, int) else pl.multiple_of(slot * T, T)
        queries = ring[2, pl.ds(start, T), :]
        grads = ring[3, pl.ds(start, T), :]
        level = lring[slot, 0:1, :]
        delta = lring[slot, 1:2, :]
        st = dot_nt(gbuf[0], queries) * scale
        dp = dot_nt(gbuf[1], grads)
        bias = bias_ref[slot]
        shift = [
            jnp.broadcast_to(bias[:, i * T:(i + 1) * T] - level, (T, T)) for i in range(4)
        ]
        p = jnp.exp(st + jnp.concatenate(shift, axis=0))
        ds = (p * (dp - delta)).astype(jnp.bfloat16)
        dv = dot_nn(p.astype(jnp.bfloat16), grads)
        dk = dot_nn(ds, queries)
        if first:
            dkv[0] = dk
            dkv[1] = dv
        else:
            dkv[0] += dk
            dkv[1] += dv

    @pl.loop(1, HALF + SKEW)
    def _(step):
        @pl.when(step < HALF)
        def _():
            forward_ring(((2, 0), (2, 1), (3, 0), (3, 1)), step)

        @pl.when(step == SKEW + 1)
        def _():
            for n in range(3):
                glse_copy(n).wait_recv()
            glse_own.wait()
            grad_q(0, T, bias_ref[0], True)
            grad_q(LAST * T, T, bias_ref[LAST], False)
            grad_kv(0, True)

        @pl.when(step > SKEW)
        def _():
            at = step - SKEW
            for way in (0, 1):
                lse_copy(way, at).wait_recv()

                @pl.when(at + 2 < HALF)
                def _():
                    lse_copy(way, at + 2).start()

            @pl.when(at + 2 == HALF)
            def _():
                lse_copy(0, at + 2).start()

            grad_q(pl.multiple_of((2 * at - 1) * T, T), 2 * T, bias_of(at), False)
            grad_kv(2 * at - 1, False)
            grad_kv(2 * at, False)

    for i in range(4):
        hsend[0, i * T:(i + 1) * T, :] = (
            jnp.transpose(dqt[:, i * T:(i + 1) * T]) * scale
        ).astype(jnp.bfloat16)

    def home_remote(t, i):
        return pltpu.make_async_remote_copy(
            src_ref=hsend.at[t, rows(i), :], dst_ref=hrecv.at[t, j],
            send_sem=h_send.at[t, i], recv_sem=h_recv.at[t, j],
            device_id=home(i), device_id_type=MESH,
        )

    def home_local(t, i):
        return pltpu.make_async_copy(hsend.at[t, rows(i), :], hrecv.at[t, j], h_recv.at[t, j])

    def send_home(t):
        for i in range(4):
            here = is_me(home(i))

            @pl.when(here)
            def _():
                home_local(t, i).start()

            @pl.when(jnp.logical_not(here))
            def _():
                home_remote(t, i).start()

    send_home(0)
    ring_last(2)
    ring_last(3)
    lse_copy(0, jnp.int32(HALF)).wait_recv()
    grad_kv(LAST, False)
    hsend[1] = (dkv[0] * scale).astype(jnp.bfloat16)
    hsend[2] = dkv[1].astype(jnp.bfloat16)
    send_home(1)
    send_home(2)

    for t in range(4):
        @pl.loop(0, 16)
        def _(h):
            @pl.when(jnp.logical_not(is_me(a2a_dest(h))))
            def _():
                a2a_remote(t, h).wait_send()

        for n in range(3):
            group_copy(t, n).wait_send()

        @pl.loop(1, HALF)
        def _(step):
            for way in (0, 1):
                for piece in range(PIECES):
                    ring_copy(t, way, step, piece).wait_send()

        for piece in range(PIECES):
            ring_copy(t, t % 2, jnp.int32(HALF), piece).wait_send()

    @pl.loop(1, HALF)
    def _(step):
        for way in (0, 1):
            lse_copy(way, step).wait_send()

    lse_copy(0, jnp.int32(HALF)).wait_send()
    for n in range(3):
        part_copy(0, n).wait_send()
        part_copy(1, n).wait_send()
        glse_copy(n).wait_send()

    @pl.when(jnp.logical_not(att_mine))
    def _():
        att_remote().wait_send()

    wait_bytes(out_ref.at[0], at_recv)
    for t in range(3):
        for i in range(4):
            wait_bytes(hrecv.at[t, i], h_recv.at[t, i])
        whole = hrecv[t, 0].astype(jnp.float32)
        for i in range(1, 4):
            whole = whole + hrecv[t, i].astype(jnp.float32)
        if t < 2:
            whole = whole * ctab[...] - pltpu.roll(whole, HD // 2, 1) * stab[...]
        out_ref[t + 1] = whole.astype(jnp.bfloat16)
    for t in range(3):
        for i in range(4):
            @pl.when(jnp.logical_not(is_me(home(i))))
            def _():
                home_remote(t, i).wait_send()


def exchange_and_attend(seq_count, toks, keys, values, query, grads, positions, views, adjacency):
    NP = seq_count // 4
    HALF = NP // 2
    T = toks
    bf, f32, i32 = jnp.bfloat16, jnp.float32, jnp.int32
    sub = keys.shape[0]
    dma = pltpu.SemaphoreType.DMA
    vmem = pl.BlockSpec(memory_space=pltpu.VMEM)
    smem = pl.BlockSpec(memory_space=pltpu.SMEM)
    anywhere = pl.BlockSpec(memory_space=pl.ANY)
    side = HD // 6 * 2
    parts = []
    for group in (HD - 2 * side, side, side):
        steps = np.arange(group // 2, dtype=np.float32)
        parts.append(np.float32(THETA) ** (np.float32(-2.0) * steps / np.float32(group)))
    freq = jnp.asarray(np.concatenate(parts * 2).astype(np.float32)[None])
    return pl.pallas_call(
        functools.partial(kernel, seq_count, toks),
        out_shape=jax.ShapeDtypeStruct((4, T, HD), bf),
        in_specs=[anywhere] * 6 + [smem, vmem],
        out_specs=vmem,
        scratch_shapes=[
            pltpu.VMEM(keys.shape, bf), pltpu.VMEM(keys.shape, bf),
            pltpu.VMEM(keys.shape, bf), pltpu.VMEM(keys.shape, bf),
            pltpu.VMEM(positions.shape, i32),
            pltpu.VMEM((seq_count, 1, T), i32),
            pltpu.VMEM((NP, 1, 4 * T), f32),
            pltpu.VMEM((T, HD), f32), pltpu.VMEM((T, HD), f32),
            dma((4,)),
            pltpu.VMEM((4, NP * T, HD), bf),
            pltpu.VMEM((4, 4 * T, HD), bf),
            pltpu.VMEM((HD, 4 * T), f32),
            pltpu.VMEM((HD, 4 * T), bf),
            pltpu.VMEM((8, 4 * T), f32),
            pltpu.VMEM((3, HD, T), bf),
            pltpu.VMEM((3, 8, T), f32),
            pltpu.VMEM((NP, 8, T), f32),
            pltpu.VMEM((8, 4 * T), f32),
            pltpu.VMEM((HD, 4 * T), f32),
            pltpu.VMEM((2, 4 * T, HD), f32),
            pltpu.VMEM((T, HD), bf),
            pltpu.VMEM((3, 4 * T, HD), bf),
            pltpu.VMEM((3, 4, T, HD), bf),
            dma((4,)), dma((4,)),
            dma((4, 3)), dma((4, 3)), dma((4,)),
            dma((4, 2)), dma((4, 2, HALF * PIECES)),
            dma((2, HALF)), dma((2, HALF)),
            dma((2, 3)), dma((2, 3)),
            dma((3,)), dma((3,)), dma,
            dma, dma,
            dma((3, 4)), dma((3, 4)),
        ],
        compiler_params=pltpu.CompilerParams(collective_id=0, has_side_effects=True),
    )(keys, values, query, grads, positions, views, adjacency, freq)


def on_device(seq_count, q_in, k_in, v_in, grad_out, positions, views, adjacency):
    T = positions.shape[1]
    out = exchange_and_attend(
        seq_count, T, k_in, v_in, q_in, grad_out,
        positions, views.reshape(seq_count, 1, T), adjacency.T,
    )
    return (out[0], out[1], out[2], out[3])


def solution(mesh):
    rows = P(("seq", "head"), None)
    in_specs = (rows, rows, rows, rows, P(None, "seq"), P(), P())
    out = P("seq", "head")
    return jax.shard_map(
        functools.partial(on_device, mesh.shape["seq"]),
        mesh=mesh, in_specs=in_specs, out_specs=(out,) * 4, check_vma=False,
    )
```
